512 devices in a mesh: lower: 16 (over y, core), upper: 8 (over z), depth: 4 (over x).
Axes of the slice: x: 4, y: 8, z: 8, core: 2. Of those that a mesh axis runs over, the one named last changes fastest.
Arguments:
- lower_vectors: bfloat16 [4, 32768, 2048], P('depth', 'lower', 'upper'), may hold values from -0.0234375 to 0.0234375
- upper_vectors: bfloat16 [4, 32768, 3072], P('depth', 'lower', 'upper'), may hold values from -6 to 6
- energy_lower: float32 [2048], P(('lower', 'depth')), may hold values from 0 to 0.5
- energy_upper: float32 [3072], P('upper'), may hold values from 1 to 2
- sym_lower: int32 [2048], P(('lower', 'depth')), may hold values from 0 to 3
- sym_upper: int32 [3072], P('upper'), may hold values from 0 to 3
- j_lower: int32 [2048], P(('lower', 'depth')), may hold values from 0 to 2
- j_upper: int32 [3072], P('upper'), may hold values from 0 to 2
Outputs:
- einstein: float32 [2048, 3072], P(('lower', 'depth'), 'upper')
The draws below stay inside these ranges and needn't reach their ends.
All inputs are finite; a program needn't handle non-finite values.
Results may differ from the reference program's by a relative error of at most 0.0003.
Values may be sent and summed in bfloat16 or wider, within the bound.
A program may use at most 64 MiB of HBM per device.

```python
import jax
import jax.numpy as jnp
from jax import lax

BASIS = 131072
NL = 2048
NU = 3072
SLAB = 32768
N_DEPTH = 4


def set_ends(values, key, least, largest):
    longest = values.shape.index(max(values.shape))
    spots = []
    for shift in (0, 1):
        where = [jax.random.randint(jax.random.fold_in(key, axis), (), 0, length) for axis, length in enumerate(values.shape)]
        where[longest] = (where[longest] + shift) % values.shape[longest]
        spots.append(tuple(where))
    return values.at[spots[0]].set(least).at[spots[1]].set(largest)


def strengthened(entries, own_key, source, target, blocks, factor):
    def block_of(axis_at):
        return (jnp.arange(entries.shape[axis_at]) // (entries.shape[axis_at] // blocks)).reshape((-1,) + (1,) * (entries.ndim - 1 - axis_at))

    near = jax.random.permutation(own_key, blocks)[block_of(target)]
    far = (block_of(target) + blocks // 2) % blocks
    return jnp.where((block_of(source) == near) | (block_of(source) == far), factor * entries, entries)


def steps_of(stream_key, shape, split, least, high):
    loudness, own = 1.0, jax.random.fold_in(stream_key, 6)
    for dim, parts in split:
        draws = jnp.exp(jax.random.uniform(jax.random.fold_in(own, dim), (parts,), jnp.float32, least / len(split), high / len(split)))
        loudness = loudness * jnp.repeat(draws, shape[dim] // parts).reshape([-1 if axis == dim else 1 for axis in range(len(shape))])
    return loudness


def scatter_about(key, shape, spread, most, shards=(), kind=jnp.bfloat16):
    array = spread * jax.random.normal(key, shape, jnp.float32)
    if shards:
        array = array * steps_of(key, shape, shards, -0.22, 0.18)
    return jnp.clip(array, -most, most).astype(kind)


def heavy_noise(own_key, extent, scale, most, pieces, heavy, held_as=jnp.bfloat16):
    result = scale * jax.random.normal(own_key, extent, jnp.float32)
    if pieces:
        result = result * steps_of(own_key, extent, pieces, -0.22, 0.18)
    return jnp.clip(strengthened(result, jax.random.fold_in(own_key, 3), *heavy), -most, most).astype(held_as)


def setup_inputs(seed: int = 0) -> dict:
    keys = jax.random.split(jax.random.key(seed), 9)
    lower_vectors = heavy_noise(keys[0], (N_DEPTH, SLAB, NL), BASIS ** -0.5, 0.0234375, ((0, 4), (1, 16), (2, 8)), (1, 2, 16, 2.0))
    upper_vectors = scatter_about(keys[1], (N_DEPTH, SLAB, NU), 1.0, 6.0, ((0, 4), (1, 16), (2, 8)))
    energy_lower = jnp.clip(0.5 * jax.random.uniform(keys[2], (NL,), jnp.float32) ** steps_of(keys[2], (NL,), ((0, 64),), -0.2, 0.2), 0.0, 0.5)
    energy_upper = jnp.clip(1.0 + 1.0 * jax.random.uniform(keys[3], (NU,), jnp.float32) ** steps_of(keys[3], (NU,), ((0, 8),), -0.2, 0.2), 1.0, 2.0)
    sym_lower = set_ends(jax.random.randint(keys[4], (NL,), 0, 4), jax.random.fold_in(keys[4], 1), 0, 3).astype(jnp.int32)
    sym_upper = set_ends(jax.random.randint(keys[5], (NU,), 0, 4), jax.random.fold_in(keys[5], 1), 0, 3).astype(jnp.int32)
    j_lower = set_ends(jax.random.randint(keys[6], (NL,), 0, 3), jax.random.fold_in(keys[6], 1), 0, 2).astype(jnp.int32)
    j_upper = set_ends(jax.random.randint(keys[7], (NU,), 0, 3), jax.random.fold_in(keys[7], 1), 0, 2).astype(jnp.int32)
    return dict(lower_vectors=lower_vectors, upper_vectors=upper_vectors, energy_lower=energy_lower, energy_upper=energy_upper, sym_lower=sym_lower, sym_upper=sym_upper, j_lower=j_lower, j_upper=j_upper)


def reference(lower_vectors, upper_vectors, energy_lower, energy_upper, sym_lower, sym_upper, j_lower, j_upper):
    moments = jnp.zeros((NL, NU), jnp.float32)
    for slab_index in range(N_DEPTH):
        lower_slab = lower_vectors[slab_index].astype(jnp.float32)
        upper_slab = upper_vectors[slab_index].astype(jnp.float32)
        moments = moments + lax.dot_general(lower_slab, upper_slab, (((0,), (0,)), ((), ())), precision=lax.Precision.HIGHEST, preferred_element_type=jnp.float32)
    parity = sym_lower % 2
    sym_rule = (sym_upper[None, :] - sym_lower[:, None]) == (1 - 2 * parity)[:, None]
    j_rule = jnp.abs(j_upper[None, :] - j_lower[:, None]) <= 1
    allowed = jnp.logical_and(sym_rule, j_rule)
    frequency = energy_upper[None, :] - energy_lower[:, None]
    weight_upper = (2 * j_upper + 1).astype(jnp.float32)
    value = frequency * frequency * frequency * (moments * moments) / weight_upper[None, :]
    return jnp.where(allowed, value, jnp.zeros_like(value))
```

```python
import functools

import jax
import jax.numpy as jnp
from jax import lax
from jax.experimental import pallas as pl
from jax.experimental.pallas import tpu as pltpu
from jax.sharding import PartitionSpec as P

MESH = pl.DeviceIdType.MESH
F32 = jnp.float32
PIECES = 4


def moments_kernel(
    lower_hbm, upper_hbm, out_ref,
    block, upper, acc, from_core, half, from_x, quarter, from_y,
    load_sem, ring_send, ring_recv, core_send, core_recv, x_send, x_recv, y_send, y_recv,
    *, n_y, n_z, n_x,
):
    li, z, x = lax.axis_index("lower"), lax.axis_index("upper"), lax.axis_index("depth")
    y, core = li // 2, lax.rem(li, 2)
    rows_all = block.shape[1]
    piece = rows_all // PIECES
    far = n_z // 2
    right, left = {"upper": lax.rem(z + 1, n_z)}, {"upper": lax.rem(z + n_z - 1, n_z)}
    sibling = {"lower": y * 2 + 1 - core}

    load_lower = pltpu.make_async_copy(lower_hbm, block.at[0], load_sem.at[0])
    load_upper = pltpu.make_async_copy(upper_hbm, upper, load_sem.at[1])
    load_lower.start()
    load_upper.start()

    barrier = pltpu.get_barrier_semaphore()
    for who in (right, left, sibling):
        pl.semaphore_signal(barrier, inc=1, device_id=who, device_id_type=MESH)
    for k in range(1, n_x):
        pl.semaphore_signal(barrier, inc=1, device_id={"depth": lax.rem(x + k, n_x)}, device_id_type=MESH)
    for k in range(1, n_y):
        pl.semaphore_signal(barrier, inc=1, device_id={"lower": lax.rem(y + k, n_y) * 2 + core}, device_id_type=MESH)
    pl.semaphore_wait(barrier, 3 + n_x - 1 + n_y - 1)

    def slot(way, d):
        if d == 0:
            return 0
        if d == far:
            return 2 * far - 1
        return d if way == 0 else far - 1 + d

    def hop(way, d, p):
        rows = pl.ds(pl.multiple_of(p * piece, piece), piece)
        to = slot(way, d)
        return pltpu.make_async_remote_copy(
            src_ref=block.at[slot(way, d - 1), rows],
            dst_ref=block.at[to, rows],
            send_sem=ring_send.at[to, p],
            recv_sem=ring_recv.at[to, p],
            device_id=right if way == 0 else left,
            device_id_type=MESH,
        )

    def goes(way, d, p):
        return d < far or (p < PIECES // 2) == (way == 0)

    load_lower.wait()
    for p in range(PIECES):
        for way in (0, 1):
            hop(way, 1, p).start()
    load_upper.wait()

    def product(b):
        return lax.dot_general(block[b], upper[...], (((0,), (0,)), ((), ())), preferred_element_type=F32)

    def core_copy(b):
        theirs = pl.ds(pl.multiple_of((1 - core) * half.shape[1], 8), half.shape[1])
        return pltpu.make_async_remote_copy(
            src_ref=acc.at[b, theirs], dst_ref=from_core.at[b],
            send_sem=core_send.at[b], recv_sem=core_recv.at[b], device_id=sibling, device_id_type=MESH,
        )

    def x_copy(b, k):
        to = lax.rem(x + k, n_x)
        n = quarter.shape[1]
        return pltpu.make_async_remote_copy(
            src_ref=half.at[b, pl.ds(pl.multiple_of(to * n, 8), n)], dst_ref=from_x.at[b, k - 1],
            send_sem=x_send.at[b, k - 1], recv_sem=x_recv.at[b, k - 1], device_id={"depth": to}, device_id_type=MESH,
        )

    def owner(b):
        if b == 0:
            return z
        if b < far:
            return lax.rem(z + n_z - b, n_z)
        if b < 2 * far - 1:
            return lax.rem(z + b - far + 1, n_z)
        return lax.rem(z + far, n_z)

    def y_copy(b, who):
        return pltpu.make_async_remote_copy(
            src_ref=quarter.at[b], dst_ref=from_y.at[y],
            send_sem=y_send.at[b], recv_sem=y_recv.at[y], device_id={"lower": who * 2 + core}, device_id_type=MESH,
        )

    def first(b):
        acc[b] = product(b)
        core_copy(b).start()

    def second(b):
        core_copy(b).wait_recv()
        mine = pl.ds(pl.multiple_of(core * half.shape[1], 8), half.shape[1])
        half[b] = acc[b, mine] + from_core[b]
        for k in range(1, n_x):
            x_copy(b, k).start()

    def third(b):
        n = quarter.shape[1]
        total = half[b, pl.ds(pl.multiple_of(x * n, 8), n)]
        for k in range(1, n_x):
            x_copy(b, k).wait_recv()
            total = total + from_x[b, k - 1]
        quarter[b] = total
        who = owner(b)

        @pl.when(who != y)
        def _():
            y_copy(b, who).start()

        @pl.when(who == y)
        def _():
            from_y[y] = quarter[b]

    groups = [[0]] + [[d, far - 1 + d] for d in range(1, far)] + [[2 * far - 1]]
    for s in range(len(groups) + 2):
        if 1 <= s < len(groups):
            for p in range(PIECES):
                for way in (0, 1):
                    if goes(way, s, p):
                        hop(way, s, p).wait_recv()
                        if s < far and goes(way, s + 1, p):
                            hop(way, s + 1, p).start()
        if s < len(groups):
            for b in groups[s]:
                first(b)
        if 1 <= s and s - 1 < len(groups):
            for b in groups[s - 1]:
                second(b)
        if 2 <= s:
            for b in groups[s - 2]:
                third(b)

    for k in range(1, n_y):
        peer = lax.rem(y + k, n_y)
        pltpu.make_async_remote_copy(
            src_ref=quarter.at[0], dst_ref=from_y.at[peer],
            send_sem=y_send.at[0], recv_sem=y_recv.at[peer], device_id={"lower": peer * 2 + core}, device_id_type=MESH,
        ).wait_recv()
    total = from_y[0]
    for k in range(1, n_y):
        total = total + from_y[k]
    out_ref[...] = total

    for d in range(1, far + 1):
        for p in range(PIECES):
            for way in (0, 1):
                if goes(way, d, p):
                    hop(way, d, p).wait_send()
    for b in range(2 * far):
        core_copy(b).wait_send()
        for k in range(1, n_x):
            x_copy(b, k).wait_send()
        who = owner(b)

        @pl.when(who != y)
        def _():
            y_copy(b, who).wait_send()


def local(
    lower_vectors, upper_vectors, energy_lower, energy_upper, sym_lower, sym_upper, j_lower, j_upper,
    *, n_y, n_z, n_x,
):
    rows, n_l = lower_vectors.shape[1:]
    n_u = upper_vectors.shape[2]
    n_out = n_l // (2 * n_x)
    vmem = pl.BlockSpec(memory_space=pltpu.VMEM)
    hbm = pl.BlockSpec(memory_space=pl.ANY)
    dma = pltpu.SemaphoreType.DMA
    moments = pl.pallas_call(
        functools.partial(moments_kernel, n_y=n_y, n_z=n_z, n_x=n_x),
        out_shape=jax.ShapeDtypeStruct((n_out, n_u), F32),
        in_specs=[hbm, hbm],
        out_specs=vmem,
        scratch_shapes=[
            pltpu.VMEM((n_z, rows, n_l), lower_vectors.dtype),
            pltpu.VMEM((rows, n_u), upper_vectors.dtype),
            pltpu.VMEM((n_z, n_l, n_u), F32),
            pltpu.VMEM((n_z, n_l // 2, n_u), F32),
            pltpu.VMEM((n_z, n_l // 2, n_u), F32),
            pltpu.VMEM((n_z, n_x - 1, n_out, n_u), F32),
            pltpu.VMEM((n_z, n_out, n_u), F32),
            pltpu.VMEM((n_y, n_out, n_u), F32),
            dma((2,)),
            dma((n_z, PIECES)), dma((n_z, PIECES)),
            dma((n_z,)), dma((n_z,)),
            dma((n_z, n_x - 1)), dma((n_z, n_x - 1)),
            dma((n_z,)), dma((n_y,)),
        ],
        compiler_params=pltpu.CompilerParams(
            collective_id=0, has_side_effects=True, vmem_limit_bytes=48 << 20
        ),
    )(lower_vectors[0], upper_vectors[0])
    parity = sym_lower % 2
    sym_rule = sym_upper[None, :] - sym_lower[:, None] == (1 - 2 * parity)[:, None]
    j_rule = jnp.abs(j_upper[None, :] - j_lower[:, None]) <= 1
    allowed = jnp.logical_and(sym_rule, j_rule)
    frequency = energy_upper[None, :] - energy_lower[:, None]
    weight_upper = (2 * j_upper + 1).astype(F32)
    value = frequency * frequency * frequency * (moments * moments) / weight_upper[None, :]
    return jnp.where(allowed, value, jnp.zeros_like(value))


def solution(mesh):
    sizes = dict(mesh.shape)
    return jax.shard_map(
        functools.partial(local, n_y=sizes["lower"] // 2, n_z=sizes["upper"], n_x=sizes["depth"]),
        mesh=mesh,
        in_specs=(
            P("depth", "lower", "upper"),
            P("depth", "lower", "upper"),
            P(("lower", "depth")),
            P("upper"),
            P(("lower", "depth")),
            P("upper"),
            P(("lower", "depth")),
            P("upper"),
        ),
        out_specs=P(("lower", "depth"), "upper"),
        check_vma=False,
    )
```

```python
import functools

import jax
import jax.numpy as jnp
from jax import lax
from jax.experimental import pallas as pl
from jax.experimental.pallas import tpu as pltpu
from jax.sharding import PartitionSpec as P

MESH = pl.DeviceIdType.MESH
F32 = jnp.float32
N_Z = 8
N_Y = 8
N_X = 4
SLICES = 4

E_AT = {1: 0, 2: 1, -1: 2, -2: 3, -3: 4, -4: 5, -5: 6}
M_AT = {1: 7, 2: 8, 3: 9, 4: 10, -1: 11, -2: 12, -3: 13}
PASS_L, NEAR_U, FAR_U, PASS_U = 14, 15, 16, 17
FLOWS = 18


def moments_kernel(
    lower_hbm, upper_hbm, out_ref,
    lower, upper, e_block, m_block, pass_l, pass_u, upper_e,
    acc, half, from_x1, second_x, from_x2, quarter, from_y, sums, from_z,
    load_sem, ring_send, ring_recv, core_send, core_recv, x1_send, x1_recv, x2_send, x2_recv, y_send, y_recv,
    z_send, z_recv,
):
    li, z, x = lax.axis_index("lower"), lax.axis_index("upper"), lax.axis_index("depth")
    y, core = li // 2, lax.rem(li, 2)
    depth = lower.shape[0] // SLICES
    n_l, n_u = lower.shape[1], upper.shape[1]
    wide = n_l // 2
    n_out = wide // N_X

    place = lax.rem(z + lax.rem(y, 2), N_Z)
    out = 2 * lax.rem(place, 2) - 1
    home_a = place // 4
    home_b = 2 + lax.rem(place + 6, N_Z) // 4
    end_a = 1 - lax.rem(place + 1, 4) // 2
    e_row = end_a * home_a + (1 - end_a) * home_b
    m_row = end_a * home_b + (1 - end_a) * home_a
    e_away = end_a * (1 - home_a) + (1 - end_a) * (5 - home_b)
    m_away = end_a * (5 - home_b) + (1 - end_a) * (1 - home_a)

    def plane(step):
        return {"upper": lax.rem(z + step + 2 * N_Z, N_Z)}

    outer, inner = plane(out), plane(-out)
    sibling = {"lower": y * 2 + 1 - core}
    flip, mirror = x + 1 - 2 * lax.rem(x, 2), 3 - x
    x1 = flip * (1 - core) + mirror * core
    x2 = mirror * (1 - core) + flip * core
    x3 = lax.rem(x + 2, N_X)

    load_lower = pltpu.make_async_copy(lower_hbm, lower, load_sem.at[0])
    load_upper = pltpu.make_async_copy(upper_hbm, upper, load_sem.at[1])
    load_upper.start()
    load_lower.start()

    barrier = pltpu.get_barrier_semaphore()
    partners = [plane(s) for s in (1, -1, 2, -2)] + [sibling, {"depth": flip}, {"depth": mirror}]
    partners += [{"lower": lax.rem(y + k, N_Y) * 2 + core} for k in range(1, N_Y)]
    for who in partners:
        pl.semaphore_signal(barrier, inc=1, device_id=who, device_id_type=MESH)
    pl.semaphore_wait(barrier, len(partners))

    def rows(k):
        return pl.ds(pl.multiple_of(k * depth, depth), depth)

    def states(p):
        return pl.ds(p * wide, wide)

    def e_piece(d, p):
        return lower.at[rows(e_row), states(p)] if d == 0 else e_block.at[E_AT[d], :, states(p)]

    def m_piece(d, p):
        return lower.at[rows(m_row), states(p)] if d == 0 else m_block.at[M_AT[d] - 7, :, states(p)]

    def ring(flow, p):
        part = depth // 2
        if flow == E_AT[1]:
            src, dst, who = lower.at[rows(e_away), states(p)], e_block.at[0, :, states(p)], outer
        elif flow == E_AT[2]:
            src, dst, who = pass_l.at[:, states(p)], e_block.at[1, :, states(p)], outer
        elif flow <= E_AT[-5]:
            src, dst, who = m_piece(flow - 2, p), e_block.at[flow, :, states(p)], inner
        elif flow <= M_AT[4]:
            src, dst, who = m_piece(7 - flow, p), m_block.at[flow - 7, :, states(p)], outer
        elif flow <= M_AT[-3]:
            src, dst, who = e_piece(flow - 11, p), m_block.at[flow - 7, :, states(p)], inner
        elif flow == PASS_L:
            src, dst, who = lower.at[rows(m_away), states(p)], pass_l.at[:, states(p)], inner
        elif flow == NEAR_U:
            src = upper.at[pl.ds(pl.multiple_of(e_away * depth + p * part, part), part)]
            dst, who = upper_e.at[pl.ds(p * part, part), pl.ds(n_u, n_u)], outer
        elif flow == FAR_U:
            src = pass_u.at[pl.ds(p * part, part)]
            dst, who = upper_e.at[pl.ds(p * part, part), pl.ds(2 * n_u, n_u)], outer
        else:
            src = upper.at[pl.ds(pl.multiple_of(m_away * depth + p * part, part), part)]
            dst, who = pass_u.at[pl.ds(p * part, part)], inner
        return pltpu.make_async_remote_copy(
            src_ref=src, dst_ref=dst, send_sem=ring_send.at[flow, p], recv_sem=ring_recv.at[flow, p],
            device_id=who, device_id_type=MESH,
        )

    def send(flow):
        for p in (0, 1):
            ring(flow, p).start()

    load_upper.wait()
    send(NEAR_U)
    send(PASS_U)
    load_lower.wait()
    send(PASS_L)
    send(M_AT[-1])
    send(E_AT[-1])
    upper_e[:, pl.ds(0, n_u)] = upper[rows(e_row), :]

    def core_copy(u):
        return pltpu.make_async_remote_copy(
            src_ref=acc.at[u, 1 - core], dst_ref=half.at[u],
            send_sem=core_send.at[u], recv_sem=core_recv.at[u], device_id=sibling, device_id_type=MESH,
        )

    def block(k):
        return pl.ds(pl.multiple_of(k * n_out, n_out), n_out)

    def x1_copy(u, k):
        return pltpu.make_async_remote_copy(
            src_ref=half.at[u, block(x1 if k == 0 else x3)], dst_ref=from_x1.at[u, k],
            send_sem=x1_send.at[u, k], recv_sem=x1_recv.at[u, k], device_id={"depth": x1}, device_id_type=MESH,
        )

    def x2_copy(u):
        return pltpu.make_async_remote_copy(
            src_ref=second_x.at[u], dst_ref=from_x2.at[u],
            send_sem=x2_send.at[u], recv_sem=x2_recv.at[u], device_id={"depth": x2}, device_id_type=MESH,
        )

    def y_copy(u, sem, slot, who):
        return pltpu.make_async_remote_copy(
            src_ref=quarter.at[u], dst_ref=from_y.at[slot],
            send_sem=y_send.at[u], recv_sem=y_recv.at[sem], device_id={"lower": who * 2 + core}, device_id_type=MESH,
        )

    units = [0, -1, 1, 2, -2, -3, 4, 3]
    wrote = {}
    fresh, running = [], []

    def root(u):
        return lax.rem(z + out * units[u] + 2 * N_Z, N_Y)

    def times(a, b):
        return lax.dot_general(a, b, (((0,), (0,)), ((), ())), preferred_element_type=F32)

    def m_product(u, d, p):
        value = times(m_piece(d, p)[...], upper[rows(m_row), :])
        if (u, p) in wrote:
            acc[u, p, :, pl.ds(0, n_u)] += value
        else:
            acc[u, p, :, pl.ds(0, n_u)] = value
        wrote[u, p] = True

    def e_full(u, d, p):
        value = times(e_piece(d, p)[...], upper_e[...])
        if (u, p) in wrote:
            acc[u, p, :, pl.ds(0, n_u)] += value[:, :n_u]
            acc[u, p, :, pl.ds(n_u, 2 * n_u)] = value[:, n_u:]
        else:
            acc[u, p] = value
        wrote[u, p] = True

    def stage(u, n):
        if n == 0:
            core_copy(u).start()
        elif n == 1:
            core_copy(u).wait_recv()
            half[u] = half[u] + acc[u, core]
            x1_copy(u, 0).start()
            x1_copy(u, 1).start()
        elif n == 2:
            x1_copy(u, 1).wait_recv()
            second_x[u] = half[u, block(x2)] + from_x1[u, 1]
            x2_copy(u).start()
            x1_copy(u, 0).wait_recv()
            quarter[u] = half[u, block(x)] + from_x1[u, 0]
        else:
            x2_copy(u).wait_recv()
            quarter[u] = quarter[u] + from_x2[u]
            who = root(u)

            @pl.when(who != y)
            def _():
                y_copy(u, y, y, who).start()

            @pl.when(who == y)
            def _():
                from_y[y] = quarter[u]

    def advance():
        for item in list(running):
            u, n = item
            stage(u, n)
            running.remove(item)
            if n < 3:
                fresh.append((u, n + 1))
        running.extend(fresh)
        fresh.clear()

    def begin(u):
        stage(u, 0)
        fresh.append((u, 1))

    def arrive(flow, onward=None):
        for p in (0, 1):
            ring(flow, p).wait_recv()
            if onward is not None:
                ring(onward, p).start()

    def e_arrive(d, onward=None, product=True):
        u = units.index(d + 8 if d < -3 else d)
        for p in (0, 1):
            ring(E_AT[d], p).wait_recv()
            if onward is not None:
                ring(onward, p).start()
            if product:
                e_full(u, d, p)

    def m_arrive(d, onward=None, onward2=None):
        u = units.index(d)
        for p in (0, 1):
            ring(M_AT[d], p).wait_recv()
            if onward is not None:
                ring(onward, p).start()
            m_product(u, d, p)

    arrive(PASS_U, FAR_U)
    send(E_AT[1])
    arrive(PASS_L, E_AT[2])
    send(M_AT[1])
    for p in (0, 1):
        m_product(0, 0, p)
    arrive(NEAR_U)
    arrive(FAR_U)
    for p in (0, 1):
        e_full(0, 0, p)
    begin(0)
    m_arrive(-1, M_AT[2])
    advance()
    e_arrive(1, M_AT[-2])
    advance()
    e_arrive(-1)
    begin(1)
    advance()
    e_arrive(2, M_AT[-3])
    advance()
    m_arrive(-2, M_AT[3])
    advance()
    m_arrive(1, E_AT[-2])
    begin(2)
    advance()
    m_arrive(-3, M_AT[4])
    advance()
    m_arrive(2, E_AT[-3])
    begin(3)
    advance()
    e_arrive(-2)
    begin(4)
    advance()
    m_arrive(3, E_AT[-4])
    advance()
    e_arrive(-3)
    begin(5)
    advance()
    m_arrive(4, E_AT[-5])
    advance()
    e_arrive(-4)
    begin(6)
    advance()
    e_arrive(-5)
    begin(7)
    advance()
    while running:
        advance()

    for k in range(1, N_Y):
        peer = lax.rem(y + k, N_Y)
        y_copy(0, peer, peer, peer).wait_recv()
    even = from_y[0] + from_y[2] + from_y[4] + from_y[6]
    odd = from_y[1] + from_y[3] + from_y[5] + from_y[7]
    sums[0] = even
    sums[1] = odd
    side = 2 * lax.rem(z, 2) - 1

    def z_copy(q, n):
        step = (side if q == 0 else -side) * n
        return pltpu.make_async_remote_copy(
            src_ref=sums.at[q, :, pl.ds(n * n_u, n_u)], dst_ref=from_z.at[q, n - 1],
            send_sem=z_send.at[q, n - 1], recv_sem=z_recv.at[q, n - 1], device_id=plane(step), device_id_type=MESH,
        )

    for n in (2, 1):
        for q in (0, 1):
            z_copy(q, n).start()
    total = even[:, :n_u] + odd[:, :n_u]
    for n in (1, 2):
        for q in (0, 1):
            z_copy(q, n).wait_recv()
            total = total + from_z[q, n - 1]
    out_ref[...] = total

    for flow in range(FLOWS):
        for p in (0, 1):
            ring(flow, p).wait_send()
    for u in range(len(units)):
        core_copy(u).wait_send()
        x1_copy(u, 0).wait_send()
        x1_copy(u, 1).wait_send()
        x2_copy(u).wait_send()
        who = root(u)

        @pl.when(who != y)
        def _():
            y_copy(u, y, y, who).wait_send()
    for n in (1, 2):
        for q in (0, 1):
            z_copy(q, n).wait_send()


def local(
    lower_vectors, upper_vectors, energy_lower, energy_upper, sym_lower, sym_upper, j_lower, j_upper
):
    rows, n_l = lower_vectors.shape[1:]
    n_u = upper_vectors.shape[2]
    n_out = n_l // (2 * N_X)
    depth = rows // SLICES
    vmem = pl.BlockSpec(memory_space=pltpu.VMEM)
    hbm = pl.BlockSpec(memory_space=pltpu.HBM)
    dma = pltpu.SemaphoreType.DMA
    kind = lower_vectors.dtype
    moments = pl.pallas_call(
        moments_kernel,
        out_shape=jax.ShapeDtypeStruct((n_out, n_u), F32),
        in_specs=[hbm, hbm],
        out_specs=vmem,
        scratch_shapes=[
            pltpu.VMEM((rows, n_l), kind),
            pltpu.VMEM((rows, n_u), kind),
            pltpu.VMEM((7, depth, n_l), kind),
            pltpu.VMEM((7, depth, n_l), kind),
            pltpu.VMEM((depth, n_l), kind),
            pltpu.VMEM((depth, n_u), kind),
            pltpu.VMEM((depth, 3 * n_u), kind),
            pltpu.VMEM((8, 2, n_l // 2, 3 * n_u), F32),
            pltpu.VMEM((8, n_l // 2, 3 * n_u), F32),
            pltpu.VMEM((8, 2, n_out, 3 * n_u), F32),
            pltpu.VMEM((8, n_out, 3 * n_u), F32),
            pltpu.VMEM((8, n_out, 3 * n_u), F32),
            pltpu.VMEM((8, n_out, 3 * n_u), F32),
            pltpu.VMEM((N_Y, n_out, 3 * n_u), F32),
            pltpu.VMEM((2, n_out, 3 * n_u), F32),
            pltpu.VMEM((2, 2, n_out, n_u), F32),
            dma((2,)),
            dma((FLOWS, 2)), dma((FLOWS, 2)),
            dma((8,)), dma((8,)),
            dma((8, 2)), dma((8, 2)),
            dma((8,)), dma((8,)),
            dma((8,)), dma((N_Y,)),
            dma((2, 2)), dma((2, 2)),
        ],
        compiler_params=pltpu.CompilerParams(
            collective_id=0, has_side_effects=True, vmem_limit_bytes=48 << 20
        ),
    )(lower_vectors[0], upper_vectors[0])
    parity = sym_lower % 2
    sym_rule = sym_upper[None, :] - sym_lower[:, None] == (1 - 2 * parity)[:, None]
    j_rule = jnp.abs(j_upper[None, :] - j_lower[:, None]) <= 1
    allowed = jnp.logical_and(sym_rule, j_rule)
    frequency = energy_upper[None, :] - energy_lower[:, None]
    weight_upper = (2 * j_upper + 1).astype(F32)
    value = frequency * frequency * frequency * (moments * moments) / weight_upper[None, :]
    return jnp.where(allowed, value, jnp.zeros_like(value))


def solution(mesh):
    return jax.shard_map(
        local,
        mesh=mesh,
        in_specs=(
            P("depth", "lower", "upper"),
            P("depth", "lower", "upper"),
            P(("lower", "depth")),
            P("upper"),
            P(("lower", "depth")),
            P("upper"),
            P(("lower", "depth")),
            P("upper"),
        ),
        out_specs=P(("lower", "depth"), "upper"),
        check_vma=False,
    )
```

```python
import functools

import jax
import jax.numpy as jnp
from jax import lax
from jax.experimental import pallas as pl
from jax.experimental.pallas import tpu as pltpu
from jax.sharding import PartitionSpec as P

MESH = pl.DeviceIdType.MESH
F32 = jnp.float32
PIECES = 4


def moments_kernel(
    lower_hbm, upper_hbm, out_ref,
    block, upper, acc, from_core, half, from_x, quarter, from_y,
    load_sem, ring_send, ring_recv, core_send, core_recv, x_send, x_recv, y_send, y_recv,
    *, n_y, n_z, n_x,
):
    li, z, x = lax.axis_index("lower"), lax.axis_index("upper"), lax.axis_index("depth")
    y, core = li // 2, lax.rem(li, 2)
    rows_all = block.shape[1]
    piece = rows_all // PIECES
    far = n_z // 2
    right, left = {"upper": lax.rem(z + 1, n_z)}, {"upper": lax.rem(z + n_z - 1, n_z)}
    sibling = {"lower": y * 2 + 1 - core}

    load_lower = pltpu.make_async_copy(lower_hbm, block.at[0], load_sem.at[0])
    load_upper = pltpu.make_async_copy(upper_hbm, upper, load_sem.at[1])
    load_lower.start()
    load_upper.start()

    barrier = pltpu.get_barrier_semaphore()
    for who in (right, left, sibling):
        pl.semaphore_signal(barrier, inc=1, device_id=who, device_id_type=MESH)
    for k in range(1, n_x):
        pl.semaphore_signal(barrier, inc=1, device_id={"depth": lax.rem(x + k, n_x)}, device_id_type=MESH)
    for k in range(1, n_y):
        pl.semaphore_signal(barrier, inc=1, device_id={"lower": lax.rem(y + k, n_y) * 2 + core}, device_id_type=MESH)
    pl.semaphore_wait(barrier, 3 + n_x - 1 + n_y - 1)

    def slot(way, d):
        if d == 0:
            return 0
        if d == far:
            return 2 * far - 1
        return d if way == 0 else far - 1 + d

    def hop(way, d, p):
        rows = pl.ds(pl.multiple_of(p * piece, piece), piece)
        to = slot(way, d)
        return pltpu.make_async_remote_copy(
            src_ref=block.at[slot(way, d - 1), rows],
            dst_ref=block.at[to, rows],
            send_sem=ring_send.at[to, p],
            recv_sem=ring_recv.at[to, p],
            device_id=right if way == 0 else left,
            device_id_type=MESH,
        )

    def goes(way, d, p):
        return d < far or (p < PIECES // 2) == (way == 0)

    load_lower.wait()
    for p in range(PIECES):
        for way in (0, 1):
            hop(way, 1, p).start()
    load_upper.wait()

    def product(b):
        return lax.dot_general(block[b], upper[...], (((0,), (0,)), ((), ())), preferred_element_type=F32)

    def core_copy(b):
        theirs = pl.ds(pl.multiple_of((1 - core) * half.shape[1], 8), half.shape[1])
        return pltpu.make_async_remote_copy(
            src_ref=acc.at[b, theirs], dst_ref=from_core.at[b],
            send_sem=core_send.at[b], recv_sem=core_recv.at[b], device_id=sibling, device_id_type=MESH,
        )

    def x_copy(b, k):
        to = lax.rem(x + k, n_x)
        n = quarter.shape[1]
        return pltpu.make_async_remote_copy(
            src_ref=half.at[b, pl.ds(pl.multiple_of(to * n, 8), n)], dst_ref=from_x.at[b, k - 1],
            send_sem=x_send.at[b, k - 1], recv_sem=x_recv.at[b, k - 1], device_id={"depth": to}, device_id_type=MESH,
        )

    def owner(b):
        if b == 0:
            return z
        if b < far:
            return lax.rem(z + n_z - b, n_z)
        if b < 2 * far - 1:
            return lax.rem(z + b - far + 1, n_z)
        return lax.rem(z + far, n_z)

    def y_copy(b, who):
        return pltpu.make_async_remote_copy(
            src_ref=quarter.at[b], dst_ref=from_y.at[y],
            send_sem=y_send.at[b], recv_sem=y_recv.at[y], device_id={"lower": who * 2 + core}, device_id_type=MESH,
        )

    def first(b):
        acc[b] = product(b)
        core_copy(b).start()

    def second(b):
        core_copy(b).wait_recv()
        mine = pl.ds(pl.multiple_of(core * half.shape[1], 8), half.shape[1])
        half[b] = acc[b, mine] + from_core[b]
        for k in range(1, n_x):
            x_copy(b, k).start()

    def third(b):
        n = quarter.shape[1]
        total = half[b, pl.ds(pl.multiple_of(x * n, 8), n)]
        for k in range(1, n_x):
            x_copy(b, k).wait_recv()
            total = total + from_x[b, k - 1]
        quarter[b] = total
        who = owner(b)

        @pl.when(who != y)
        def _():
            y_copy(b, who).start()

        @pl.when(who == y)
        def _():
            from_y[y] = quarter[b]

    groups = [[0]] + [[d, far - 1 + d] for d in range(1, far)] + [[2 * far - 1]]
    for s in range(len(groups) + 2):
        if 1 <= s < len(groups):
            for p in range(PIECES):
                for way in (0, 1):
                    if goes(way, s, p):
                        hop(way, s, p).wait_recv()
                        if s < far and goes(way, s + 1, p):
                            hop(way, s + 1, p).start()
        if s < len(groups):
            for b in groups[s]:
                first(b)
        if 1 <= s and s - 1 < len(groups):
            for b in groups[s - 1]:
                second(b)
        if 2 <= s:
            for b in groups[s - 2]:
                third(b)

    for k in range(1, n_y):
        peer = lax.rem(y + k, n_y)
        pltpu.make_async_remote_copy(
            src_ref=quarter.at[0], dst_ref=from_y.at[peer],
            send_sem=y_send.at[0], recv_sem=y_recv.at[peer], device_id={"lower": peer * 2 + core}, device_id_type=MESH,
        ).wait_recv()
    total = from_y[0]
    for k in range(1, n_y):
        total = total + from_y[k]
    out_ref[...] = total

    for d in range(1, far + 1):
        for p in range(PIECES):
            for way in (0, 1):
                if goes(way, d, p):
                    hop(way, d, p).wait_send()
    for b in range(2 * far):
        core_copy(b).wait_send()
        for k in range(1, n_x):
            x_copy(b, k).wait_send()
        who = owner(b)

        @pl.when(who != y)
        def _():
            y_copy(b, who).wait_send()


def local(
    lower_vectors, upper_vectors, energy_lower, energy_upper, sym_lower, sym_upper, j_lower, j_upper,
    *, n_y, n_z, n_x,
):
    rows, n_l = lower_vectors.shape[1:]
    n_u = upper_vectors.shape[2]
    n_out = n_l // (2 * n_x)
    vmem = pl.BlockSpec(memory_space=pltpu.VMEM)
    hbm = pl.BlockSpec(memory_space=pltpu.HBM)
    dma = pltpu.SemaphoreType.DMA
    moments = pl.pallas_call(
        functools.partial(moments_kernel, n_y=n_y, n_z=n_z, n_x=n_x),
        out_shape=jax.ShapeDtypeStruct((n_out, n_u), F32),
        in_specs=[hbm, hbm],
        out_specs=vmem,
        scratch_shapes=[
            pltpu.VMEM((n_z, rows, n_l), lower_vectors.dtype),
            pltpu.VMEM((rows, n_u), upper_vectors.dtype),
            pltpu.VMEM((n_z, n_l, n_u), F32),
            pltpu.VMEM((n_z, n_l // 2, n_u), F32),
            pltpu.VMEM((n_z, n_l // 2, n_u), F32),
            pltpu.VMEM((n_z, n_x - 1, n_out, n_u), F32),
            pltpu.VMEM((n_z, n_out, n_u), F32),
            pltpu.VMEM((n_y, n_out, n_u), F32),
            dma((2,)),
            dma((n_z, PIECES)), dma((n_z, PIECES)),
            dma((n_z,)), dma((n_z,)),
            dma((n_z, n_x - 1)), dma((n_z, n_x - 1)),
            dma((n_z,)), dma((n_y,)),
        ],
        compiler_params=pltpu.CompilerParams(
            collective_id=0, has_side_effects=True, vmem_limit_bytes=60 << 20
        ),
    )(lower_vectors[0], upper_vectors[0])
    parity = sym_lower % 2
    sym_rule = sym_upper[None, :] - sym_lower[:, None] == (1 - 2 * parity)[:, None]
    j_rule = jnp.abs(j_upper[None, :] - j_lower[:, None]) <= 1
    allowed = jnp.logical_and(sym_rule, j_rule)
    frequency = energy_upper[None, :] - energy_lower[:, None]
    weight_upper = (2 * j_upper + 1).astype(F32)
    value = frequency * frequency * frequency * (moments * moments) / weight_upper[None, :]
    return jnp.where(allowed, value, jnp.zeros_like(value))


def solution(mesh):
    sizes = dict(mesh.shape)
    return jax.shard_map(
        functools.partial(local, n_y=sizes["lower"] // 2, n_z=sizes["upper"], n_x=sizes["depth"]),
        mesh=mesh,
        in_specs=(
            P("depth", "lower", "upper"),
            P("depth", "lower", "upper"),
            P(("lower", "depth")),
            P("upper"),
            P(("lower", "depth")),
            P("upper"),
            P(("lower", "depth")),
            P("upper"),
        ),
        out_specs=P(("lower", "depth"), "upper"),
        check_vma=False,
    )
```

```python
import functools

import jax
import jax.numpy as jnp
from jax import lax
from jax.experimental import pallas as pl
from jax.experimental.pallas import tpu as pltpu
from jax.sharding import PartitionSpec as P

MESH = pl.DeviceIdType.MESH
F32 = jnp.float32
N_Z = 8
N_Y = 8
N_X = 4
SLICES = 4

E_AT = {1: 0, 2: 1, -1: 2, -2: 3, -3: 4, -4: 5, -5: 6}
M_AT = {1: 7, 2: 8, 3: 9, 4: 10, -1: 11, -2: 12, -3: 13}
PASS_L, NEAR_U, FAR_U, PASS_U = 14, 15, 16, 17
FLOWS = 18
HOPS = (
    (M_AT, -1, M_AT[2]), (E_AT, 1, M_AT[-2]), (E_AT, -1, None), (E_AT, 2, M_AT[-3]), (M_AT, -2, M_AT[3]),
    (M_AT, 1, E_AT[-2]), (M_AT, -3, M_AT[4]), (M_AT, 2, E_AT[-3]), (E_AT, -2, None), (M_AT, 3, E_AT[-4]),
    (E_AT, -3, None), (M_AT, 4, E_AT[-5]), (E_AT, -4, None), (E_AT, -5, None),
)
LAST = 7
PLAN = (
    (),
    ((0, 1),),
    (),
    (),
    (),
    (),
    (),
    ((0, 2), (1, 1)),
    (),
    ((0, 3),),
    (),
    (),
    (),
    ((1, 2), (2, 1)),
    (),
    ((0, 4), (1, 3)),
    (),
    ((3, 1), (2, 2)),
    (),
    ((1, 4),),
    (),
    ((4, 1), (3, 2)),
    (),
    ((2, 3), (5, 1)),
    (),
    ((4, 2),),
    ((3, 3), (2, 4), (6, 1)),
    ((5, 2), (4, 3)),
    (),
    ((3, 4), (6, 2), (5, 3), (4, 4), (7, 3), (5, 4), (6, 3), (7, 4), (6, 4)),
)


def moments_kernel(
    lower_hbm, upper_hbm, out_ref,
    lower, upper, e_block, m_block, pass_l, pass_u, upper_e,
    acc, half, from_x1, second_x, from_x2, quarter, from_xd, from_y, part, finals,
    load_sem, ring_send, ring_recv, core_send, core_recv, x1_send, x1_recv, x2_send, x2_recv, y_send, y_recv,
    xd_send, xd_recv, final_send, final_recv,
):
    li, z, x = lax.axis_index("lower"), lax.axis_index("upper"), lax.axis_index("depth")
    y, core = li // 2, lax.rem(li, 2)
    depth = lower.shape[0] // SLICES
    n_l, n_u = lower.shape[1], upper.shape[1]
    wide = n_l // 2
    n_out = wide // N_X
    n_group = n_out // 4

    place = lax.rem(z + lax.rem(y, 2), N_Z)
    out = 2 * lax.rem(place, 2) - 1
    home_a = place // 4
    home_b = 2 + lax.rem(place + 6, N_Z) // 4
    end_a = 1 - lax.rem(place + 1, 4) // 2
    e_row = end_a * home_a + (1 - end_a) * home_b
    m_row = end_a * home_b + (1 - end_a) * home_a
    e_away = end_a * (1 - home_a) + (1 - end_a) * (5 - home_b)
    m_away = end_a * (5 - home_b) + (1 - end_a) * (1 - home_a)

    def plane(step):
        return {"upper": lax.rem(z + step + 2 * N_Z, N_Z)}

    outer, inner = plane(out), plane(-out)
    sibling = {"lower": y * 2 + 1 - core}
    flip, mirror = x + 1 - 2 * lax.rem(x, 2), 3 - x
    x1 = flip * (1 - core) + mirror * core
    x2 = mirror * (1 - core) + flip * core
    x3 = lax.rem(x + 2, N_X)

    load_lower = pltpu.make_async_copy(lower_hbm, lower, load_sem.at[0])
    load_upper = pltpu.make_async_copy(upper_hbm, upper, load_sem.at[1])
    load_upper.start()
    load_lower.start()

    barrier = pltpu.get_barrier_semaphore()
    side = 2 * lax.rem(z, 2) - 1
    partners = [inner, sibling] + [{"depth": lax.rem(x + k, N_X)} for k in range(1, N_X)]
    for k in range(N_Y):
        peer = lax.rem(y + k, N_Y)
        at = side * (1 - 2 * lax.rem(peer, 2))
        for step in (0, at, -2 * at) if k else (at, -2 * at):
            partners.append({"lower": peer * 2 + core, "upper": lax.rem(z + step + 2 * N_Z, N_Z)})
    for who in partners:
        pl.semaphore_signal(barrier, inc=1, device_id=who, device_id_type=MESH)
    pl.semaphore_wait(barrier, len(partners))

    def rows(k):
        return pl.ds(pl.multiple_of(k * depth, depth), depth)

    def states(p):
        return pl.ds(p * wide, wide)

    def e_piece(d, p):
        return lower.at[rows(e_row), states(p)] if d == 0 else e_block.at[E_AT[d], :, states(p)]

    def m_piece(d, p):
        return lower.at[rows(m_row), states(p)] if d == 0 else m_block.at[M_AT[d] - 7, :, states(p)]

    def ring(flow, p):
        part = depth // 2
        if flow == E_AT[1]:
            src, dst, who = lower.at[rows(e_away), states(p)], e_block.at[0, :, states(p)], outer
        elif flow == E_AT[2]:
            src, dst, who = pass_l.at[:, states(p)], e_block.at[1, :, states(p)], outer
        elif flow <= E_AT[-5]:
            src, dst, who = m_piece(flow - 2, p), e_block.at[flow, :, states(p)], inner
        elif flow <= M_AT[4]:
            src, dst, who = m_piece(7 - flow, p), m_block.at[flow - 7, :, states(p)], outer
        elif flow <= M_AT[-3]:
            src, dst, who = e_piece(flow - 11, p), m_block.at[flow - 7, :, states(p)], inner
        elif flow == PASS_L:
            src, dst, who = lower.at[rows(m_away), states(p)], pass_l.at[:, states(p)], inner
        elif flow == NEAR_U:
            src = upper.at[pl.ds(pl.multiple_of(e_away * depth + p * part, part), part)]
            dst, who = upper_e.at[pl.ds(p * part, part), pl.ds(n_u, n_u)], outer
        elif flow == FAR_U:
            src = pass_u.at[pl.ds(p * part, part)]
            dst, who = upper_e.at[pl.ds(p * part, part), pl.ds(2 * n_u, n_u)], outer
        else:
            src = upper.at[pl.ds(pl.multiple_of(m_away * depth + p * part, part), part)]
            dst, who = pass_u.at[pl.ds(p * part, part)], inner
        return pltpu.make_async_remote_copy(
            src_ref=src, dst_ref=dst, send_sem=ring_send.at[flow, p], recv_sem=ring_recv.at[flow, p],
            device_id=who, device_id_type=MESH,
        )

    def send(flow):
        for p in (0, 1):
            ring(flow, p).start()

    load_upper.wait()
    send(NEAR_U)
    send(PASS_U)
    load_lower.wait()
    send(PASS_L)
    send(M_AT[-1])
    send(E_AT[-1])
    upper_e[:, pl.ds(0, n_u)] = upper[rows(e_row), :]

    def core_copy(u):
        return pltpu.make_async_remote_copy(
            src_ref=acc.at[u, 1 - core], dst_ref=half.at[u],
            send_sem=core_send.at[u], recv_sem=core_recv.at[u], device_id=sibling, device_id_type=MESH,
        )

    def group(k):
        return pl.ds(pl.multiple_of(k * n_group, n_group), n_group)

    def block(k):
        return pl.ds(pl.multiple_of(k * n_out, n_out), n_out)

    def x1_copy(u, k):
        return pltpu.make_async_remote_copy(
            src_ref=half.at[u, block(x1 if k == 0 else x3)], dst_ref=from_x1.at[u, k],
            send_sem=x1_send.at[u, k], recv_sem=x1_recv.at[u, k], device_id={"depth": x1}, device_id_type=MESH,
        )

    def x2_copy(u):
        return pltpu.make_async_remote_copy(
            src_ref=second_x.at[u], dst_ref=from_x2.at[u],
            send_sem=x2_send.at[u], recv_sem=x2_recv.at[u], device_id={"depth": x2}, device_id_type=MESH,
        )

    def y_copy(u, k):
        to = lax.rem(y + 2 * k, N_Y)
        return pltpu.make_async_remote_copy(
            src_ref=quarter.at[u, group(to // 2)], dst_ref=from_y.at[u, k - 1],
            send_sem=y_send.at[u, k - 1], recv_sem=y_recv.at[u, k - 1], device_id={"lower": to * 2 + core},
            device_id_type=MESH,
        )

    def xd_copy(k):
        to = lax.rem(x + k, N_X)
        return pltpu.make_async_remote_copy(
            src_ref=half.at[LAST, block(to)], dst_ref=from_xd.at[k - 1],
            send_sem=xd_send.at[k - 1], recv_sem=xd_recv.at[k - 1], device_id={"depth": to}, device_id_type=MESH,
        )

    def final_copy(u, j, who, of):
        step = j * out
        return pltpu.make_async_remote_copy(
            src_ref=part.at[u, j], dst_ref=finals.at[j, lax.rem(of, 2), group(of // 2)],
            send_sem=final_send.at[u, j], recv_sem=final_recv.at[j, of],
            device_id={"lower": who * 2 + core, "upper": lax.rem(z + step + 2 * N_Z, N_Z)}, device_id_type=MESH,
        )

    units = [0, -1, 1, 2, -2, -3, 4, 3]
    wrote = {}

    def root(u):
        return lax.rem(z + out * units[u] + 2 * N_Z, N_Y)

    def times(a, b):
        return lax.dot_general(a, b, (((0,), (0,)), ((), ())), preferred_element_type=F32)

    def m_product(u, d, p):
        value = times(m_piece(d, p)[...], upper[rows(m_row), :])
        if (u, p) in wrote:
            acc[u, p, :, pl.ds(0, n_u)] += value
        else:
            acc[u, p, :, pl.ds(0, n_u)] = value
        wrote[u, p] = True

    def e_full(u, d, p):
        value = times(e_piece(d, p)[...], upper_e[...])
        if (u, p) in wrote:
            acc[u, p, :, pl.ds(0, n_u)] += value[:, :n_u]
            acc[u, p, :, pl.ds(n_u, 2 * n_u)] = value[:, n_u:]
        else:
            acc[u, p] = value
        wrote[u, p] = True

    def stage(u, n):
        if n == 0:
            core_copy(u).start()
        elif n == 1:
            core_copy(u).wait_recv()
            half[u] = half[u] + acc[u, core]
            if u == LAST:
                for k in (1, 3, 2):
                    xd_copy(k).start()
            else:
                x1_copy(u, 1).start()
                x1_copy(u, 0).start()
        elif n == 2:
            x1_copy(u, 1).wait_recv()
            second_x[u] = half[u, block(x2)] + from_x1[u, 1]
            x2_copy(u).start()
            x1_copy(u, 0).wait_recv()
            quarter[u] = half[u, block(x)] + from_x1[u, 0]
        elif n == 3:
            if u == LAST:
                value = half[u, block(x)]
                for k in (1, 3, 2):
                    xd_copy(k).wait_recv()
                    value = value + from_xd[k - 1]
                quarter[u] = value
            else:
                x2_copy(u).wait_recv()
                quarter[u] = quarter[u] + from_x2[u]
            for k in (2, 1, 3):
                y_copy(u, k).start()
        else:
            value = quarter[u, group(y // 2)]
            for k in (1, 3, 2):
                y_copy(u, k).wait_recv()
                value = value + from_y[u, k - 1]
            for j in range(3):
                part[u, j] = value[:, j * n_u : (j + 1) * n_u]
            who = root(u)
            final_copy(u, 2, who, y).start()
            final_copy(u, 1, who, y).start()

            @pl.when(who != y)
            def _():
                final_copy(u, 0, who, y).start()

            @pl.when(who == y)
            def _():
                finals[0, lax.rem(y, 2), group(y // 2)] = part[u, 0]

    def due(n):
        for u, k in PLAN[n]:
            stage(u, k)

    def arrive(flow, onward=None):
        for p in (0, 1):
            ring(flow, p).wait_recv()
            if onward is not None:
                ring(onward, p).start()

    arrive(PASS_U, FAR_U)
    send(E_AT[1])
    arrive(PASS_L, E_AT[2])
    send(M_AT[1])
    for p in (0, 1):
        m_product(0, 0, p)
    arrive(NEAR_U)
    arrive(FAR_U)
    for p in (0, 1):
        e_full(0, 0, p)
    stage(0, 0)
    due(0)
    for n, (kind, d, onward) in enumerate(HOPS):
        u = units.index(d + 8 if d < -3 else d)
        for p in (0, 1):
            ring(kind[d], p).wait_recv()
            if onward is not None:
                ring(onward, p).start()
            done = (u, p) in wrote
            if kind is E_AT:
                e_full(u, d, p)
            else:
                m_product(u, d, p)
            if u == LAST and done:
                pl.when(core == 1 - p)(functools.partial(stage, u, 0))
            elif done and p == 1:
                stage(u, 0)
            due(2 * n + p + 1)
            if u == LAST and done:
                pl.when(core == p)(functools.partial(stage, u, 1))
    due(2 * len(HOPS) + 1)

    for j in range(3):
        for k in range(1 if j == 0 else 0, N_Y):
            peer = lax.rem(y + k, N_Y)
            final_copy(0, j, peer, peer).wait_recv()
    total = finals[0, 0] + finals[0, 1]
    for j in (1, 2):
        total = total + (finals[j, 0] + finals[j, 1])
    out_ref[...] = total

    for flow in range(FLOWS):
        for p in (0, 1):
            ring(flow, p).wait_send()
    for u in range(len(units)):
        core_copy(u).wait_send()
        if u == LAST:
            for k in (1, 2, 3):
                xd_copy(k).wait_send()
        else:
            x1_copy(u, 0).wait_send()
            x1_copy(u, 1).wait_send()
            x2_copy(u).wait_send()
        for k in (1, 2, 3):
            y_copy(u, k).wait_send()
        who = root(u)
        final_copy(u, 1, who, y).wait_send()
        final_copy(u, 2, who, y).wait_send()

        @pl.when(who != y)
        def _():
            final_copy(u, 0, who, y).wait_send()


def local(
    lower_vectors, upper_vectors, energy_lower, energy_upper, sym_lower, sym_upper, j_lower, j_upper
):
    rows, n_l = lower_vectors.shape[1:]
    n_u = upper_vectors.shape[2]
    n_out = n_l // (2 * N_X)
    depth = rows // SLICES
    vmem = pl.BlockSpec(memory_space=pltpu.VMEM)
    hbm = pl.BlockSpec(memory_space=pltpu.HBM)
    dma = pltpu.SemaphoreType.DMA
    kind = lower_vectors.dtype
    moments = pl.pallas_call(
        moments_kernel,
        out_shape=jax.ShapeDtypeStruct((n_out, n_u), F32),
        in_specs=[hbm, hbm],
        out_specs=vmem,
        scratch_shapes=[
            pltpu.VMEM((rows, n_l), kind),
            pltpu.VMEM((rows, n_u), kind),
            pltpu.VMEM((7, depth, n_l), kind),
            pltpu.VMEM((7, depth, n_l), kind),
            pltpu.VMEM((depth, n_l), kind),
            pltpu.VMEM((depth, n_u), kind),
            pltpu.VMEM((depth, 3 * n_u), kind),
            pltpu.VMEM((8, 2, n_l // 2, 3 * n_u), F32),
            pltpu.VMEM((8, n_l // 2, 3 * n_u), F32),
            pltpu.VMEM((8, 2, n_out, 3 * n_u), F32),
            pltpu.VMEM((8, n_out, 3 * n_u), F32),
            pltpu.VMEM((8, n_out, 3 * n_u), F32),
            pltpu.VMEM((8, n_out, 3 * n_u), F32),
            pltpu.VMEM((3, n_out, 3 * n_u), F32),
            pltpu.VMEM((8, 3, n_out // 4, 3 * n_u), F32),
            pltpu.VMEM((8, 3, n_out // 4, n_u), F32),
            pltpu.VMEM((3, 2, n_out, n_u), F32),
            dma((2,)),
            dma((FLOWS, 2)), dma((FLOWS, 2)),
            dma((8,)), dma((8,)),
            dma((8, 2)), dma((8, 2)),
            dma((8,)), dma((8,)),
            dma((8, 3)), dma((8, 3)),
            dma((3,)), dma((3,)),
            dma((8, 3)), dma((3, N_Y)),
        ],
        compiler_params=pltpu.CompilerParams(
            collective_id=0, has_side_effects=True, vmem_limit_bytes=60 << 20
        ),
    )(lower_vectors[0], upper_vectors[0])
    parity = sym_lower % 2
    sym_rule = sym_upper[None, :] - sym_lower[:, None] == (1 - 2 * parity)[:, None]
    j_rule = jnp.abs(j_upper[None, :] - j_lower[:, None]) <= 1
    allowed = jnp.logical_and(sym_rule, j_rule)
    frequency = energy_upper[None, :] - energy_lower[:, None]
    weight_upper = (2 * j_upper + 1).astype(F32)
    value = frequency * frequency * frequency * (moments * moments) / weight_upper[None, :]
    return jnp.where(allowed, value, jnp.zeros_like(value))


def solution(mesh):
    return jax.shard_map(
        local,
        mesh=mesh,
        in_specs=(
            P("depth", "lower", "upper"),
            P("depth", "lower", "upper"),
            P(("lower", "depth")),
            P("upper"),
            P(("lower", "depth")),
            P("upper"),
            P(("lower", "depth")),
            P("upper"),
        ),
        out_specs=P(("lower", "depth"), "upper"),
        check_vma=False,
    )
```

```python
import functools

import jax
import jax.numpy as jnp
from jax import lax
from jax.experimental import pallas as pl
from jax.experimental.pallas import tpu as pltpu
from jax.sharding import PartitionSpec as P

MESH = pl.DeviceIdType.MESH
F32 = jnp.float32
N_Z = 8
N_Y = 8
N_X = 4
SLICES = 4

E_AT = {1: 0, 2: 1, -1: 2, -2: 3, -3: 4, -4: 5, -5: 6}
M_AT = {1: 7, 2: 8, 3: 9, 4: 10, -1: 11, -2: 12, -3: 13}
PASS_L, NEAR_U, FAR_U, PASS_U = 14, 15, 16, 17
FLOWS = 18
HOPS = (
    (M_AT, -1, M_AT[2]), (E_AT, 1, M_AT[-2]), (E_AT, -1, None), (M_AT, 1, E_AT[-2]), (M_AT, -2, M_AT[3]),
    (E_AT, 2, M_AT[-3]), (E_AT, -2, None), (M_AT, 2, E_AT[-3]), (M_AT, -3, M_AT[4]), (M_AT, 3, E_AT[-4]),
    (E_AT, -3, None), (M_AT, 4, E_AT[-5]), (E_AT, -4, None), (E_AT, -5, None),
)
DIRECT = (6, 7)
SPLIT = (1, 2, 3, 4, 5, 6, 7)
PLAN = (
    (),
    ((0, 1),),
    (),
    (),
    (),
    (),
    (),
    ((0, 2),),
    (),
    (),
    (),
    ((0, 3),),
    (),
    ((1, 2),),
    (),
    ((0, 4), (2, 2)),
    (),
    ((1, 3),),
    (),
    ((2, 3),),
    (),
    ((1, 4), (3, 2)),
    (),
    ((2, 4), (4, 2)),
    (),
    ((3, 3),),
    ((4, 3),),
    ((3, 4), (5, 2)),
    (),
    ((4, 4), (6, 3), (5, 3), (6, 4), (7, 3), (5, 4), (7, 4)),
)


def moments_kernel(
    lower_hbm, upper_hbm, out_ref,
    lower, upper, e_block, m_block, pass_l, pass_u, upper_e,
    acc, half, from_x1, second_x, from_x2, quarter, from_xd, from_y, part, finals,
    load_sem, ring_send, ring_recv, core_send, core_recv, x1_send, x1_recv, x2_send, x2_recv, y_send, y_recv,
    xd_send, xd_recv, final_send, final_recv,
):
    li, z, x = lax.axis_index("lower"), lax.axis_index("upper"), lax.axis_index("depth")
    y, core = li // 2, lax.rem(li, 2)
    depth = lower.shape[0] // SLICES
    n_l, n_u = lower.shape[1], upper.shape[1]
    wide = n_l // 2
    n_out = wide // N_X
    n_group = n_out // 4

    place = lax.rem(z + lax.rem(y, 2), N_Z)
    out = 2 * lax.rem(place, 2) - 1
    home_a = place // 4
    home_b = 2 + lax.rem(place + 6, N_Z) // 4
    end_a = 1 - lax.rem(place + 1, 4) // 2
    e_row = end_a * home_a + (1 - end_a) * home_b
    m_row = end_a * home_b + (1 - end_a) * home_a
    e_away = end_a * (1 - home_a) + (1 - end_a) * (5 - home_b)
    m_away = end_a * (5 - home_b) + (1 - end_a) * (1 - home_a)

    def plane(step):
        return {"upper": lax.rem(z + step + 2 * N_Z, N_Z)}

    outer, inner = plane(out), plane(-out)
    sibling = {"lower": y * 2 + 1 - core}
    flip, mirror = x + 1 - 2 * lax.rem(x, 2), 3 - x
    x1 = flip * (1 - core) + mirror * core
    x2 = mirror * (1 - core) + flip * core
    x3 = lax.rem(x + 2, N_X)

    load_lower = pltpu.make_async_copy(lower_hbm, lower, load_sem.at[0])
    load_upper = pltpu.make_async_copy(upper_hbm, upper, load_sem.at[1])
    load_upper.start()
    load_lower.start()

    barrier = pltpu.get_barrier_semaphore()
    side = 2 * lax.rem(z, 2) - 1
    partners = [inner, sibling] + [{"depth": lax.rem(x + k, N_X)} for k in range(1, N_X)]
    for k in range(N_Y):
        peer = lax.rem(y + k, N_Y)
        at = side * (1 - 2 * lax.rem(peer, 2))
        for step in (0, at, -2 * at) if k else (at, -2 * at):
            partners.append({"lower": peer * 2 + core, "upper": lax.rem(z + step + 2 * N_Z, N_Z)})
    for who in partners:
        pl.semaphore_signal(barrier, inc=1, device_id=who, device_id_type=MESH)
    pl.semaphore_wait(barrier, len(partners))

    def rows(k):
        return pl.ds(pl.multiple_of(k * depth, depth), depth)

    def states(p):
        return pl.ds(p * wide, wide)

    def e_piece(d, p):
        return lower.at[rows(e_row), states(p)] if d == 0 else e_block.at[E_AT[d], :, states(p)]

    def m_piece(d, p):
        return lower.at[rows(m_row), states(p)] if d == 0 else m_block.at[M_AT[d] - 7, :, states(p)]

    def ring(flow, p):
        part = depth // 2
        if flow == E_AT[1]:
            src, dst, who = lower.at[rows(e_away), states(p)], e_block.at[0, :, states(p)], outer
        elif flow == E_AT[2]:
            src, dst, who = pass_l.at[:, states(p)], e_block.at[1, :, states(p)], outer
        elif flow <= E_AT[-5]:
            src, dst, who = m_piece(flow - 2, p), e_block.at[flow, :, states(p)], inner
        elif flow <= M_AT[4]:
            src, dst, who = m_piece(7 - flow, p), m_block.at[flow - 7, :, states(p)], outer
        elif flow <= M_AT[-3]:
            src, dst, who = e_piece(flow - 11, p), m_block.at[flow - 7, :, states(p)], inner
        elif flow == PASS_L:
            src, dst, who = lower.at[rows(m_away), states(p)], pass_l.at[:, states(p)], inner
        elif flow == NEAR_U:
            src = upper.at[pl.ds(pl.multiple_of(e_away * depth + p * part, part), part)]
            dst, who = upper_e.at[pl.ds(p * part, part), pl.ds(n_u, n_u)], outer
        elif flow == FAR_U:
            src = pass_u.at[pl.ds(p * part, part)]
            dst, who = upper_e.at[pl.ds(p * part, part), pl.ds(2 * n_u, n_u)], outer
        else:
            src = upper.at[pl.ds(pl.multiple_of(m_away * depth + p * part, part), part)]
            dst, who = pass_u.at[pl.ds(p * part, part)], inner
        return pltpu.make_async_remote_copy(
            src_ref=src, dst_ref=dst, send_sem=ring_send.at[flow, p], recv_sem=ring_recv.at[flow, p],
            device_id=who, device_id_type=MESH,
        )

    def send(flow):
        for p in (0, 1):
            ring(flow, p).start()

    load_upper.wait()
    send(NEAR_U)
    send(PASS_U)
    load_lower.wait()
    send(PASS_L)
    send(M_AT[-1])
    send(E_AT[-1])
    upper_e[:, pl.ds(0, n_u)] = upper[rows(e_row), :]

    def core_copy(u):
        return pltpu.make_async_remote_copy(
            src_ref=acc.at[u, 1 - core], dst_ref=half.at[u],
            send_sem=core_send.at[u], recv_sem=core_recv.at[u], device_id=sibling, device_id_type=MESH,
        )

    def group(k):
        return pl.ds(pl.multiple_of(k * n_group, n_group), n_group)

    def block(k):
        return pl.ds(pl.multiple_of(k * n_out, n_out), n_out)

    def x1_copy(u, k):
        return pltpu.make_async_remote_copy(
            src_ref=half.at[u, block(x1 if k == 0 else x3)], dst_ref=from_x1.at[u, k],
            send_sem=x1_send.at[u, k], recv_sem=x1_recv.at[u, k], device_id={"depth": x1}, device_id_type=MESH,
        )

    def x2_copy(u):
        return pltpu.make_async_remote_copy(
            src_ref=second_x.at[u], dst_ref=from_x2.at[u],
            send_sem=x2_send.at[u], recv_sem=x2_recv.at[u], device_id={"depth": x2}, device_id_type=MESH,
        )

    def y_copy(u, k):
        to = lax.rem(y + 2 * k, N_Y)
        return pltpu.make_async_remote_copy(
            src_ref=quarter.at[u, group(to // 2)], dst_ref=from_y.at[u, k - 1],
            send_sem=y_send.at[u, k - 1], recv_sem=y_recv.at[u, k - 1], device_id={"lower": to * 2 + core},
            device_id_type=MESH,
        )

    def xd_copy(u, k):
        to = lax.rem(x + k, N_X)
        return pltpu.make_async_remote_copy(
            src_ref=half.at[u, block(to)], dst_ref=from_xd.at[u, k - 1],
            send_sem=xd_send.at[u, k - 1], recv_sem=xd_recv.at[u, k - 1], device_id={"depth": to}, device_id_type=MESH,
        )

    def final_copy(u, j, who, of):
        step = j * out
        return pltpu.make_async_remote_copy(
            src_ref=part.at[u, j], dst_ref=finals.at[j, lax.rem(of, 2), group(of // 2)],
            send_sem=final_send.at[u, j], recv_sem=final_recv.at[j, of],
            device_id={"lower": who * 2 + core, "upper": lax.rem(z + step + 2 * N_Z, N_Z)}, device_id_type=MESH,
        )

    units = [0, -1, 1, -2, 2, -3, 4, 3]
    wrote = {}

    def root(u):
        return lax.rem(z + out * units[u] + 2 * N_Z, N_Y)

    def times(a, b):
        return lax.dot_general(a, b, (((0,), (0,)), ((), ())), preferred_element_type=F32)

    def m_product(u, d, p):
        value = times(m_piece(d, p)[...], upper[rows(m_row), :])
        if (u, p) in wrote:
            acc[u, p, :, pl.ds(0, n_u)] += value
        else:
            acc[u, p, :, pl.ds(0, n_u)] = value
        wrote[u, p] = True

    def e_full(u, d, p):
        value = times(e_piece(d, p)[...], upper_e[...])
        if (u, p) in wrote:
            acc[u, p, :, pl.ds(0, n_u)] += value[:, :n_u]
            acc[u, p, :, pl.ds(n_u, 2 * n_u)] = value[:, n_u:]
        else:
            acc[u, p] = value
        wrote[u, p] = True

    def stage(u, n):
        if n == 0:
            core_copy(u).start()
        elif n == 1:
            core_copy(u).wait_recv()
            half[u] = half[u] + acc[u, core]
            if u in DIRECT:
                for k in (1, 3, 2):
                    xd_copy(u, k).start()
            else:
                x1_copy(u, 1).start()
                x1_copy(u, 0).start()
        elif n == 2:
            x1_copy(u, 1).wait_recv()
            second_x[u] = half[u, block(x2)] + from_x1[u, 1]
            x2_copy(u).start()
            x1_copy(u, 0).wait_recv()
            quarter[u] = half[u, block(x)] + from_x1[u, 0]
        elif n == 3:
            if u in DIRECT:
                value = half[u, block(x)]
                for k in (1, 3, 2):
                    xd_copy(u, k).wait_recv()
                    value = value + from_xd[u, k - 1]
                quarter[u] = value
            else:
                x2_copy(u).wait_recv()
                quarter[u] = quarter[u] + from_x2[u]
            for k in (2, 1, 3):
                y_copy(u, k).start()
        else:
            value = quarter[u, group(y // 2)]
            for k in (1, 3, 2):
                y_copy(u, k).wait_recv()
                value = value + from_y[u, k - 1]
            for j in range(3):
                part[u, j] = value[:, j * n_u : (j + 1) * n_u]
            who = root(u)
            final_copy(u, 2, who, y).start()
            final_copy(u, 1, who, y).start()

            @pl.when(who != y)
            def _():
                final_copy(u, 0, who, y).start()

            @pl.when(who == y)
            def _():
                finals[0, lax.rem(y, 2), group(y // 2)] = part[u, 0]

    def due(n):
        for u, k in PLAN[n]:
            stage(u, k)

    def arrive(flow, onward=None):
        for p in (0, 1):
            ring(flow, p).wait_recv()
            if onward is not None:
                ring(onward, p).start()

    arrive(PASS_U, FAR_U)
    send(E_AT[1])
    send(M_AT[1])
    arrive(PASS_L, E_AT[2])
    for p in (0, 1):
        m_product(0, 0, p)
    arrive(NEAR_U)
    arrive(FAR_U)
    for p in (0, 1):
        e_full(0, 0, p)
    stage(0, 0)
    due(0)
    for n, (kind, d, onward) in enumerate(HOPS):
        u = units.index(d + 8 if d < -3 else d)
        for p in (0, 1):
            ring(kind[d], p).wait_recv()
            if onward is not None:
                ring(onward, p).start()
            done = (u, p) in wrote
            if kind is E_AT:
                e_full(u, d, p)
            else:
                m_product(u, d, p)
            if u in SPLIT and done:
                pl.when(core == 1 - p)(functools.partial(stage, u, 0))
            elif done and p == 1:
                stage(u, 0)
            due(2 * n + p + 1)
            if u in SPLIT and done:
                pl.when(core == p)(functools.partial(stage, u, 1))
    due(2 * len(HOPS) + 1)

    for j in range(3):
        for k in range(1 if j == 0 else 0, N_Y):
            peer = lax.rem(y + k, N_Y)
            final_copy(0, j, peer, peer).wait_recv()
    total = finals[0, 0] + finals[0, 1]
    for j in (1, 2):
        total = total + (finals[j, 0] + finals[j, 1])
    out_ref[...] = total

    for flow in range(FLOWS):
        for p in (0, 1):
            ring(flow, p).wait_send()
    for u in range(len(units)):
        core_copy(u).wait_send()
        if u in DIRECT:
            for k in (1, 2, 3):
                xd_copy(u, k).wait_send()
        else:
            x1_copy(u, 0).wait_send()
            x1_copy(u, 1).wait_send()
            x2_copy(u).wait_send()
        for k in (1, 2, 3):
            y_copy(u, k).wait_send()
        who = root(u)
        final_copy(u, 1, who, y).wait_send()
        final_copy(u, 2, who, y).wait_send()

        @pl.when(who != y)
        def _():
            final_copy(u, 0, who, y).wait_send()


def local(
    lower_vectors, upper_vectors, energy_lower, energy_upper, sym_lower, sym_upper, j_lower, j_upper
):
    rows, n_l = lower_vectors.shape[1:]
    n_u = upper_vectors.shape[2]
    n_out = n_l // (2 * N_X)
    depth = rows // SLICES
    vmem = pl.BlockSpec(memory_space=pltpu.VMEM)
    hbm = pl.BlockSpec(memory_space=pltpu.HBM)
    dma = pltpu.SemaphoreType.DMA
    kind = lower_vectors.dtype
    moments = pl.pallas_call(
        moments_kernel,
        out_shape=jax.ShapeDtypeStruct((n_out, n_u), F32),
        in_specs=[hbm, hbm],
        out_specs=vmem,
        scratch_shapes=[
            pltpu.VMEM((rows, n_l), kind),
            pltpu.VMEM((rows, n_u), kind),
            pltpu.VMEM((7, depth, n_l), kind),
            pltpu.VMEM((7, depth, n_l), kind),
            pltpu.VMEM((depth, n_l), kind),
            pltpu.VMEM((depth, n_u), kind),
            pltpu.VMEM((depth, 3 * n_u), kind),
            pltpu.VMEM((8, 2, n_l // 2, 3 * n_u), F32),
            pltpu.VMEM((8, n_l // 2, 3 * n_u), F32),
            pltpu.VMEM((8, 2, n_out, 3 * n_u), F32),
            pltpu.VMEM((8, n_out, 3 * n_u), F32),
            pltpu.VMEM((8, n_out, 3 * n_u), F32),
            pltpu.VMEM((8, n_out, 3 * n_u), F32),
            pltpu.VMEM((8, 3, n_out, 3 * n_u), F32),
            pltpu.VMEM((8, 3, n_out // 4, 3 * n_u), F32),
            pltpu.VMEM((8, 3, n_out // 4, n_u), F32),
            pltpu.VMEM((3, 2, n_out, n_u), F32),
            dma((2,)),
            dma((FLOWS, 2)), dma((FLOWS, 2)),
            dma((8,)), dma((8,)),
            dma((8, 2)), dma((8, 2)),
            dma((8,)), dma((8,)),
            dma((8, 3)), dma((8, 3)),
            dma((8, 3)), dma((8, 3)),
            dma((8, 3)), dma((3, N_Y)),
        ],
        compiler_params=pltpu.CompilerParams(
            collective_id=0, has_side_effects=True, vmem_limit_bytes=60 << 20
        ),
    )(lower_vectors[0], upper_vectors[0])
    parity = sym_lower % 2
    sym_rule = sym_upper[None, :] - sym_lower[:, None] == (1 - 2 * parity)[:, None]
    j_rule = jnp.abs(j_upper[None, :] - j_lower[:, None]) <= 1
    allowed = jnp.logical_and(sym_rule, j_rule)
    frequency = energy_upper[None, :] - energy_lower[:, None]
    weight_upper = (2 * j_upper + 1).astype(F32)
    value = frequency * frequency * frequency * (moments * moments) / weight_upper[None, :]
    return jnp.where(allowed, value, jnp.zeros_like(value))


def solution(mesh):
    return jax.shard_map(
        local,
        mesh=mesh,
        in_specs=(
            P("depth", "lower", "upper"),
            P("depth", "lower", "upper"),
            P(("lower", "depth")),
            P("upper"),
            P(("lower", "depth")),
            P("upper"),
            P(("lower", "depth")),
            P("upper"),
        ),
        out_specs=P(("lower", "depth"), "upper"),
        check_vma=False,
    )
```

```python
import functools

import jax
import jax.numpy as jnp
from jax import lax
from jax.experimental import pallas as pl
from jax.experimental.pallas import tpu as pltpu
from jax.sharding import PartitionSpec as P

MESH = pl.DeviceIdType.MESH
F32 = jnp.float32
N_Z = 8
N_Y = 8
N_X = 4
SLICES = 4

E_AT = {1: 0, 2: 1, -1: 2, -2: 3, -3: 4, -4: 5, -5: 6}
M_AT = {1: 7, 2: 8, 3: 9, 4: 10, -1: 11, -2: 12, -3: 13}
PASS_L, NEAR_U, FAR_U, PASS_U = 14, 15, 16, 17
FLOWS = 18
HOPS = (
    (M_AT, -1, M_AT[2]), (E_AT, 1, M_AT[-2]), (E_AT, -1, None), (M_AT, 1, E_AT[-2]), (M_AT, -2, M_AT[3]),
    (E_AT, 2, M_AT[-3]), (E_AT, -2, None), (M_AT, 2, E_AT[-3]), (M_AT, -3, M_AT[4]), (M_AT, 3, E_AT[-4]),
    (E_AT, -3, None), (M_AT, 4, E_AT[-5]), (E_AT, -4, None), (E_AT, -5, None),
)
DIRECT = (6, 7)
SPLIT = (1, 2, 3, 4, 5, 6, 7)
PLAN = (
    (),
    ((0, 1),),
    (),
    (),
    (),
    (),
    (),
    ((0, 2),),
    (),
    (),
    (),
    ((0, 3),),
    (),
    ((1, 2),),
    (),
    ((0, 4), (2, 2)),
    (),
    ((1, 3),),
    (),
    ((2, 3),),
    (),
    ((1, 4), (3, 2)),
    (),
    ((2, 4), (4, 2)),
    (),
    ((3, 3),),
    ((4, 3),),
    ((3, 4), (5, 2)),
    (),
    ((6, 3), (5, 3), (4, 4), (7, 3), (6, 4), (5, 4), (7, 4)),
)


def moments_kernel(
    lower_hbm, upper_hbm, out_ref,
    lower, upper, e_block, m_block, pass_l, pass_u, upper_e,
    acc, half, from_x1, second_x, from_x2, quarter, from_xd, from_y, part, finals,
    load_sem, ring_send, ring_recv, core_send, core_recv, x1_send, x1_recv, x2_send, x2_recv, y_send, y_recv,
    xd_send, xd_recv, final_send, final_recv,
):
    li, z, x = lax.axis_index("lower"), lax.axis_index("upper"), lax.axis_index("depth")
    y, core = li // 2, lax.rem(li, 2)
    depth = lower.shape[0] // SLICES
    n_l, n_u = lower.shape[1], upper.shape[1]
    wide = n_l // 2
    n_out = wide // N_X
    n_group = n_out // 4

    place = lax.rem(z + lax.rem(y, 2), N_Z)
    out = 2 * lax.rem(place, 2) - 1
    home_a = place // 4
    home_b = 2 + lax.rem(place + 6, N_Z) // 4
    end_a = 1 - lax.rem(place + 1, 4) // 2
    e_row = end_a * home_a + (1 - end_a) * home_b
    m_row = end_a * home_b + (1 - end_a) * home_a
    e_away = end_a * (1 - home_a) + (1 - end_a) * (5 - home_b)
    m_away = end_a * (5 - home_b) + (1 - end_a) * (1 - home_a)

    def plane(step):
        return {"upper": lax.rem(z + step + 2 * N_Z, N_Z)}

    outer, inner = plane(out), plane(-out)
    sibling = {"lower": y * 2 + 1 - core}
    flip, mirror = x + 1 - 2 * lax.rem(x, 2), 3 - x
    x1 = flip * (1 - core) + mirror * core
    x2 = mirror * (1 - core) + flip * core
    x3 = lax.rem(x + 2, N_X)

    load_lower = pltpu.make_async_copy(lower_hbm, lower, load_sem.at[0])
    load_upper = pltpu.make_async_copy(upper_hbm, upper, load_sem.at[1])
    load_upper.start()
    load_lower.start()

    barrier = pltpu.get_barrier_semaphore()
    side = 2 * lax.rem(z, 2) - 1
    partners = [inner, sibling] + [{"depth": lax.rem(x + k, N_X)} for k in range(1, N_X)]
    for k in range(N_Y):
        peer = lax.rem(y + k, N_Y)
        at = side * (1 - 2 * lax.rem(peer, 2))
        for step in (0, at, -2 * at) if k else (at, -2 * at):
            partners.append({"lower": peer * 2 + core, "upper": lax.rem(z + step + 2 * N_Z, N_Z)})
    for who in partners:
        pl.semaphore_signal(barrier, inc=1, device_id=who, device_id_type=MESH)
    pl.semaphore_wait(barrier, len(partners))

    def rows(k):
        return pl.ds(pl.multiple_of(k * depth, depth), depth)

    def states(p):
        return pl.ds(p * wide, wide)

    def e_piece(d, p):
        return lower.at[rows(e_row), states(p)] if d == 0 else e_block.at[E_AT[d], :, states(p)]

    def m_piece(d, p):
        return lower.at[rows(m_row), states(p)] if d == 0 else m_block.at[M_AT[d] - 7, :, states(p)]

    def ring(flow, p):
        part = depth // 2
        if flow == E_AT[1]:
            src, dst, who = lower.at[rows(e_away), states(p)], e_block.at[0, :, states(p)], outer
        elif flow == E_AT[2]:
            src, dst, who = pass_l.at[:, states(p)], e_block.at[1, :, states(p)], outer
        elif flow <= E_AT[-5]:
            src, dst, who = m_piece(flow - 2, p), e_block.at[flow, :, states(p)], inner
        elif flow <= M_AT[4]:
            src, dst, who = m_piece(7 - flow, p), m_block.at[flow - 7, :, states(p)], outer
        elif flow <= M_AT[-3]:
            src, dst, who = e_piece(flow - 11, p), m_block.at[flow - 7, :, states(p)], inner
        elif flow == PASS_L:
            src, dst, who = lower.at[rows(m_away), states(p)], pass_l.at[:, states(p)], inner
        elif flow == NEAR_U:
            src = upper.at[pl.ds(pl.multiple_of(e_away * depth + p * part, part), part)]
            dst, who = upper_e.at[pl.ds(p * part, part), pl.ds(n_u, n_u)], outer
        elif flow == FAR_U:
            src = pass_u.at[pl.ds(p * part, part)]
            dst, who = upper_e.at[pl.ds(p * part, part), pl.ds(2 * n_u, n_u)], outer
        else:
            src = upper.at[pl.ds(pl.multiple_of(m_away * depth + p * part, part), part)]
            dst, who = pass_u.at[pl.ds(p * part, part)], inner
        return pltpu.make_async_remote_copy(
            src_ref=src, dst_ref=dst, send_sem=ring_send.at[flow, p], recv_sem=ring_recv.at[flow, p],
            device_id=who, device_id_type=MESH,
        )

    def send(flow):
        for p in (0, 1):
            ring(flow, p).start()

    load_upper.wait()
    send(NEAR_U)
    send(PASS_U)
    load_lower.wait()
    send(PASS_L)
    send(M_AT[-1])
    send(E_AT[-1])
    upper_e[:, pl.ds(0, n_u)] = upper[rows(e_row), :]

    def core_copy(u):
        return pltpu.make_async_remote_copy(
            src_ref=acc.at[u, 1 - core], dst_ref=half.at[u],
            send_sem=core_send.at[u], recv_sem=core_recv.at[u], device_id=sibling, device_id_type=MESH,
        )

    def group(k):
        return pl.ds(pl.multiple_of(k * n_group, n_group), n_group)

    def block(k):
        return pl.ds(pl.multiple_of(k * n_out, n_out), n_out)

    def x1_copy(u, k):
        return pltpu.make_async_remote_copy(
            src_ref=half.at[u, block(x1 if k == 0 else x3)], dst_ref=from_x1.at[u, k],
            send_sem=x1_send.at[u, k], recv_sem=x1_recv.at[u, k], device_id={"depth": x1}, device_id_type=MESH,
        )

    def x2_copy(u):
        return pltpu.make_async_remote_copy(
            src_ref=second_x.at[u], dst_ref=from_x2.at[u],
            send_sem=x2_send.at[u], recv_sem=x2_recv.at[u], device_id={"depth": x2}, device_id_type=MESH,
        )

    def y_copy(u, k):
        to = lax.rem(y + 2 * k, N_Y)
        return pltpu.make_async_remote_copy(
            src_ref=quarter.at[u, group(to // 2)], dst_ref=from_y.at[u, k - 1],
            send_sem=y_send.at[u, k - 1], recv_sem=y_recv.at[u, k - 1], device_id={"lower": to * 2 + core},
            device_id_type=MESH,
        )

    def xd_copy(u, k):
        to = lax.rem(x + k, N_X)
        return pltpu.make_async_remote_copy(
            src_ref=half.at[u, block(to)], dst_ref=from_xd.at[u, k - 1],
            send_sem=xd_send.at[u, k - 1], recv_sem=xd_recv.at[u, k - 1], device_id={"depth": to}, device_id_type=MESH,
        )

    def final_copy(u, j, who, of):
        step = j * out
        return pltpu.make_async_remote_copy(
            src_ref=part.at[u, j], dst_ref=finals.at[j, lax.rem(of, 2), group(of // 2)],
            send_sem=final_send.at[u, j], recv_sem=final_recv.at[j, of],
            device_id={"lower": who * 2 + core, "upper": lax.rem(z + step + 2 * N_Z, N_Z)}, device_id_type=MESH,
        )

    units = [0, -1, 1, -2, 2, -3, 4, 3]
    wrote = {}

    def root(u):
        return lax.rem(z + out * units[u] + 2 * N_Z, N_Y)

    def times(a, b):
        return lax.dot_general(a, b, (((0,), (0,)), ((), ())), preferred_element_type=F32)

    def m_product(u, d, p):
        value = times(m_piece(d, p)[...], upper[rows(m_row), :])
        if (u, p) in wrote:
            acc[u, p, :, pl.ds(0, n_u)] += value
        else:
            acc[u, p, :, pl.ds(0, n_u)] = value
        wrote[u, p] = True

    def e_full(u, d, p):
        value = times(e_piece(d, p)[...], upper_e[...])
        if (u, p) in wrote:
            acc[u, p, :, pl.ds(0, n_u)] += value[:, :n_u]
            acc[u, p, :, pl.ds(n_u, 2 * n_u)] = value[:, n_u:]
        else:
            acc[u, p] = value
        wrote[u, p] = True

    def stage(u, n):
        if n == 0:
            core_copy(u).start()
        elif n == 1:
            core_copy(u).wait_recv()
            half[u] = half[u] + acc[u, core]
            if u in DIRECT:
                for k in (1, 3, 2):
                    xd_copy(u, k).start()
            else:
                x1_copy(u, 1).start()
                x1_copy(u, 0).start()
        elif n == 2:
            x1_copy(u, 1).wait_recv()
            second_x[u] = half[u, block(x2)] + from_x1[u, 1]
            x2_copy(u).start()
            x1_copy(u, 0).wait_recv()
            quarter[u] = half[u, block(x)] + from_x1[u, 0]
        elif n == 3:
            if u in DIRECT:
                value = half[u, block(x)]
                for k in (1, 3, 2):
                    xd_copy(u, k).wait_recv()
                    value = value + from_xd[u, k - 1]
                quarter[u] = value
            else:
                x2_copy(u).wait_recv()
                quarter[u] = quarter[u] + from_x2[u]
            for k in (2, 1, 3):
                y_copy(u, k).start()
        else:
            value = quarter[u, group(y // 2)]
            for k in (1, 3, 2):
                y_copy(u, k).wait_recv()
                value = value + from_y[u, k - 1]
            for j in range(3):
                part[u, j] = value[:, j * n_u : (j + 1) * n_u]
            who = root(u)
            final_copy(u, 2, who, y).start()
            final_copy(u, 1, who, y).start()

            @pl.when(who != y)
            def _():
                final_copy(u, 0, who, y).start()

            @pl.when(who == y)
            def _():
                finals[0, lax.rem(y, 2), group(y // 2)] = part[u, 0]

    def due(n):
        for u, k in PLAN[n]:
            stage(u, k)

    def arrive(flow, onward=None):
        for p in (0, 1):
            ring(flow, p).wait_recv()
            if onward is not None:
                ring(onward, p).start()

    arrive(PASS_U, FAR_U)
    send(E_AT[1])
    send(M_AT[1])
    arrive(PASS_L, E_AT[2])
    for p in (0, 1):
        m_product(0, 0, p)
    arrive(NEAR_U)
    arrive(FAR_U)
    for p in (0, 1):
        e_full(0, 0, p)
    stage(0, 0)
    due(0)
    for n, (kind, d, onward) in enumerate(HOPS):
        u = units.index(d + 8 if d < -3 else d)
        for p in (0, 1):
            ring(kind[d], p).wait_recv()
            if onward is not None:
                ring(onward, p).start()
            done = (u, p) in wrote
            if kind is E_AT:
                e_full(u, d, p)
            else:
                m_product(u, d, p)
            if u in SPLIT and done:
                pl.when(core == 1 - p)(functools.partial(stage, u, 0))
            elif done and p == 1:
                stage(u, 0)
            due(2 * n + p + 1)
            if u in SPLIT and done:
                pl.when(core == p)(functools.partial(stage, u, 1))
    due(2 * len(HOPS) + 1)

    for j in range(3):
        for k in range(1 if j == 0 else 0, N_Y):
            peer = lax.rem(y + k, N_Y)
            final_copy(0, j, peer, peer).wait_recv()
    total = finals[0, 0] + finals[0, 1]
    for j in (1, 2):
        total = total + (finals[j, 0] + finals[j, 1])
    out_ref[...] = total

    for flow in range(FLOWS):
        for p in (0, 1):
            ring(flow, p).wait_send()
    for u in range(len(units)):
        core_copy(u).wait_send()
        if u in DIRECT:
            for k in (1, 2, 3):
                xd_copy(u, k).wait_send()
        else:
            x1_copy(u, 0).wait_send()
            x1_copy(u, 1).wait_send()
            x2_copy(u).wait_send()
        for k in (1, 2, 3):
            y_copy(u, k).wait_send()
        who = root(u)
        final_copy(u, 1, who, y).wait_send()
        final_copy(u, 2, who, y).wait_send()

        @pl.when(who != y)
        def _():
            final_copy(u, 0, who, y).wait_send()


def local(
    lower_vectors, upper_vectors, energy_lower, energy_upper, sym_lower, sym_upper, j_lower, j_upper
):
    rows, n_l = lower_vectors.shape[1:]
    n_u = upper_vectors.shape[2]
    n_out = n_l // (2 * N_X)
    depth = rows // SLICES
    vmem = pl.BlockSpec(memory_space=pltpu.VMEM)
    hbm = pl.BlockSpec(memory_space=pltpu.HBM)
    dma = pltpu.SemaphoreType.DMA
    kind = lower_vectors.dtype
    moments = pl.pallas_call(
        moments_kernel,
        out_shape=jax.ShapeDtypeStruct((n_out, n_u), F32),
        in_specs=[hbm, hbm],
        out_specs=vmem,
        scratch_shapes=[
            pltpu.VMEM((rows, n_l), kind),
            pltpu.VMEM((rows, n_u), kind),
            pltpu.VMEM((7, depth, n_l), kind),
            pltpu.VMEM((7, depth, n_l), kind),
            pltpu.VMEM((depth, n_l), kind),
            pltpu.VMEM((depth, n_u), kind),
            pltpu.VMEM((depth, 3 * n_u), kind),
            pltpu.VMEM((8, 2, n_l // 2, 3 * n_u), F32),
            pltpu.VMEM((8, n_l // 2, 3 * n_u), F32),
            pltpu.VMEM((8, 2, n_out, 3 * n_u), F32),
            pltpu.VMEM((8, n_out, 3 * n_u), F32),
            pltpu.VMEM((8, n_out, 3 * n_u), F32),
            pltpu.VMEM((8, n_out, 3 * n_u), F32),
            pltpu.VMEM((8, 3, n_out, 3 * n_u), F32),
            pltpu.VMEM((8, 3, n_out // 4, 3 * n_u), F32),
            pltpu.VMEM((8, 3, n_out // 4, n_u), F32),
            pltpu.VMEM((3, 2, n_out, n_u), F32),
            dma((2,)),
            dma((FLOWS, 2)), dma((FLOWS, 2)),
            dma((8,)), dma((8,)),
            dma((8, 2)), dma((8, 2)),
            dma((8,)), dma((8,)),
            dma((8, 3)), dma((8, 3)),
            dma((8, 3)), dma((8, 3)),
            dma((8, 3)), dma((3, N_Y)),
        ],
        compiler_params=pltpu.CompilerParams(
            collective_id=0, has_side_effects=True, vmem_limit_bytes=60 << 20
        ),
    )(lower_vectors[0], upper_vectors[0])
    parity = sym_lower % 2
    sym_rule = sym_upper[None, :] - sym_lower[:, None] == (1 - 2 * parity)[:, None]
    j_rule = jnp.abs(j_upper[None, :] - j_lower[:, None]) <= 1
    allowed = jnp.logical_and(sym_rule, j_rule)
    frequency = energy_upper[None, :] - energy_lower[:, None]
    weight_upper = (2 * j_upper + 1).astype(F32)
    value = frequency * frequency * frequency * (moments * moments) / weight_upper[None, :]
    return jnp.where(allowed, value, jnp.zeros_like(value))


def solution(mesh):
    return jax.shard_map(
        local,
        mesh=mesh,
        in_specs=(
            P("depth", "lower", "upper"),
            P("depth", "lower", "upper"),
            P(("lower", "depth")),
            P("upper"),
            P(("lower", "depth")),
            P("upper"),
            P(("lower", "depth")),
            P("upper"),
        ),
        out_specs=P(("lower", "depth"), "upper"),
        check_vma=False,
    )
```
